256 devices in a mesh: dp: 64 (over x, z, core), grp: 4 (over y).
Axes of the slice: x: 4, y: 4, z: 8, core: 2. Of those that a mesh axis runs over, the one named last changes fastest.
Arguments:
- embeddings: bfloat16 [8192, 64, 1024], P('dp', None, 'grp'), may hold values from -17 to 17
- lengths: int32 [8192], P('dp'), may hold values from 1 to 64
- parent_slot: int32 [8192], P('dp'), may hold values from 0 to 8191, as said below
- centroids: bfloat16 [8192, 16, 1024], P('dp', None, 'grp'), may hold values from -17 to 17
Outputs:
- refined: bfloat16 [8192, 16, 1024], P('dp', None, 'grp')
The draws below stay inside these ranges and needn't reach their ends.
Inputs may be any that keep to these rules, and one draw needn't show every extreme that they name: `parent_slot`: each parent has its own slot; slot // 128 is the index of dp that keeps that parent's centroids; the parents of one index of dp are kept by exactly 32 indices of dp, 4 by each. Rows past lengths[p] in a block are padding.
All inputs are finite; a program needn't handle non-finite values.
Results may differ from the reference program's by a relative error of at most 0.0057.
Values may be sent and summed in bfloat16 or wider, within the bound.
A program may use at most 128 MiB of HBM per device.

```python
import math
import jax
import jax.numpy as jnp
from jax import lax

D = 1024
CHILDREN = 16
BLOCK = 64
ITERS = 2
PAR_DEV = 128
PARENTS = 8192
CAP = 4
N_DP = 64


def draw_scaled(key, shape):
    key_scale, key_core, key_column = jax.random.split(key, 3)
    width = shape[-1]
    position = jnp.arange(width, dtype=jnp.float32) / width
    jitter = jax.random.uniform(key_column, (width,), jnp.float32, 0.6, 1.4)
    column = jnp.exp(math.log(8.0) * (position - 1.0)) * jitter
    spread = jnp.exp(jax.random.uniform(key_scale, shape[:-1] + (1,), jnp.float32, math.log(0.3), math.log(3.0)))
    core = jnp.clip(jax.random.normal(key_core, shape, jnp.float32), -4.0, 4.0)
    return core * spread * column


def draw_embeddings(key, part):
    return draw_scaled(jax.random.fold_in(key, 11), (PARENTS, BLOCK, D)).astype(jnp.bfloat16)


def draw_centroids(key, part):
    return draw_scaled(jax.random.fold_in(key, 23), (PARENTS, CHILDREN, D)).astype(jnp.bfloat16)


def draw_parent_slot(key, part):
    key_shift, random_purpose_seed, key_local = jax.random.split(jax.random.fold_in(key, 37), 3)
    offsets = jnp.arange(N_DP, dtype=jnp.int32)
    forced = (offsets == 1) | (offsets == N_DP - 1) | (offsets == N_DP // 2)
    shift_score = jax.random.randint(key_shift, (N_DP,), 0, 1 << 20, dtype=jnp.int32)
    shift_score = jnp.where(forced, -1, shift_score) * N_DP + offsets
    shifts = jnp.argsort(shift_score)[:N_DP // 2].astype(jnp.int32)
    within_rank = jnp.arange(PAR_DEV, dtype=jnp.int32)[None, :]
    role_score = jax.random.randint(random_purpose_seed, (N_DP, PAR_DEV), 0, 1 << 16, dtype=jnp.int32) * PAR_DEV + within_rank
    role = jnp.argsort(role_score, axis=1).astype(jnp.int32)
    group = role // CAP
    inside_parent_position = role % CAP
    device = jnp.arange(N_DP, dtype=jnp.int32)[:, None]
    holder = (device + shifts[group]) % N_DP
    local_score = jax.random.randint(key_local, (N_DP, PAR_DEV), 0, 1 << 16, dtype=jnp.int32) * PAR_DEV + within_rank
    local_order = jnp.argsort(local_score, axis=1).astype(jnp.int32)
    local_slot = local_order[holder, group * CAP + inside_parent_position]
    return (holder * PAR_DEV + local_slot).reshape(-1).astype(jnp.int32)


def set_ends(result, rng, least, largest):
    shape = result.shape
    index_at = [jax.random.randint(jax.random.fold_in(rng, axis), (), 0, shape[axis]) for axis in range(len(shape))]
    result = result.at[tuple(index_at)].set(least)
    longest = shape.index(max(shape))
    index_at[longest] = (index_at[longest] + 1) % shape[longest]
    return result.at[tuple(index_at)].set(largest)


def setup_inputs(seed: int = 0) -> dict:
    key_list = jax.random.split(jax.random.key(seed), 5)
    embeddings = draw_embeddings(jax.random.fold_in(key_list[4], 71), 0)
    lengths = set_ends(jax.random.randint(key_list[1], (PARENTS,), 1, BLOCK + 1), jax.random.fold_in(key_list[1], 1), 1, BLOCK).astype(jnp.int32)
    parent_slot = draw_parent_slot(jax.random.fold_in(key_list[4], 71), 0)
    centroids = draw_centroids(jax.random.fold_in(key_list[4], 71), 0)
    return {"embeddings": embeddings, "lengths": lengths, "parent_slot": parent_slot, "centroids": centroids}


assignment_sharpness = 0.02
prior_weight = 1.0
epsilon = 1e-06

def refine_group(vectors, block_lengths, start):
    highest = lax.Precision.HIGHEST
    vec_f = vectors.astype(jnp.float32)
    sample_norm_multiplier = lax.rsqrt(lax.optimization_barrier(jnp.sum(vec_f * vec_f, axis=-1)) + epsilon)
    live_rows = jnp.arange(BLOCK)[None, :] < block_lengths[:, None]
    current = start
    for step in range(ITERS):
        cur_f = current.astype(jnp.float32)
        cluster_mean_norm_multiplier = lax.rsqrt(lax.optimization_barrier(jnp.sum(cur_f * cur_f, axis=-1)) + epsilon)
        cosine_similarity_matrix = jnp.einsum('pkd,pbd->pkb', cur_f, vec_f, precision=highest)
        membership_logits = cosine_similarity_matrix * cluster_mean_norm_multiplier[:, :, None] * sample_norm_multiplier[:, None, :] / assignment_sharpness
        raised = jnp.exp(membership_logits)
        weights = jnp.where(live_rows[:, None, :], raised / lax.optimization_barrier(jnp.sum(raised, axis=1, keepdims=True)), 0.0).astype(jnp.bfloat16)
        weight_f = weights.astype(jnp.float32)
        moments = jnp.einsum('pkb,pbd->pkd', weight_f, vec_f, precision=highest)
        totals = lax.optimization_barrier(jnp.sum(weight_f, axis=2))
        current = ((moments + prior_weight * cur_f) / (totals + prior_weight)[:, :, None]).astype(jnp.bfloat16)
    return current

def reference(embeddings, lengths, parent_slot, centroids):
    groups = PARENTS // PAR_DEV
    start = jnp.take(centroids, parent_slot, axis=0)
    grouped = (embeddings.reshape(groups, PAR_DEV, BLOCK, D), lengths.reshape(groups, PAR_DEV), start.reshape(groups, PAR_DEV, CHILDREN, D))
    updated_output = lax.map(lambda item: refine_group(item[0], item[1], item[2]), grouped)
    updated_output = updated_output.reshape(PARENTS, CHILDREN, D)
    return jnp.zeros_like(centroids).at[parent_slot].set(updated_output)
```

```python
import functools

import jax
import jax.numpy as jnp
from jax import lax
from jax.experimental import pallas as pl
from jax.experimental.pallas import tpu as pltpu
from jax.sharding import PartitionSpec as P

ITERS = 2
CAP = 4
LANES = 128

sharpness = 0.02
prior = 1.0
epsilon = 1e-06

MESH = pl.DeviceIdType.MESH


def wait_bytes(ref, sem):
    pltpu.make_async_copy(ref, ref, sem).wait()


def dot_t(left, right):
    return lax.dot_general(
        left, right, (((1,), (1,)), ((), ())), preferred_element_type=jnp.float32
    )


def kernel(
    n, groups, stride,
    msg, meta, posmap, x_hbm, cent_hbm,
    out, slots_out,
    x, cent, slotrecv, slot_s, c0send, c0recv, start, osend, cur,
    ysend, yrecv, wbuf, rsend, rrecv, rscale,
    load_sem, slot_send, slot_recv, c0_send, c0_recv, o_send, o_recv, own_sem,
    r_send, r_recv, y_send, y_recv, w_send, w_recv,
):
    parents, block, width = x.shape
    children = cent.shape[1]
    chunk = parents // CAP
    per_owner = chunk // 2 // groups
    me = lax.axis_index("dp")
    g = lax.axis_index("grp")

    def peer(i):
        return lax.rem(me + lax.rem(i * stride, n), n)

    def mate(i):
        return lax.rem(g + i, groups)

    load_x = pltpu.make_async_copy(x_hbm, x, load_sem.at[0])
    load_c = pltpu.make_async_copy(cent_hbm, cent, load_sem.at[1])
    load_c.start()
    load_x.start()

    barrier = pltpu.get_barrier_semaphore()

    @pl.loop(1, n)
    def _(i):
        pl.semaphore_signal(barrier, inc=1, device_id=(peer(i), g), device_id_type=MESH)

    @pl.loop(1, groups)
    def _(i):
        pl.semaphore_signal(barrier, inc=1, device_id=(me, mate(i)), device_id_type=MESH)

    pl.semaphore_wait(barrier, n - 1 + groups - 1)

    @pl.loop(1, n)
    def _(i):
        p = peer(i)
        pltpu.make_async_remote_copy(
            src_ref=msg.at[p], dst_ref=slotrecv.at[me],
            send_sem=slot_send, recv_sem=slot_recv,
            device_id=(p, g), device_id_type=MESH,
        ).start()

    slotrecv[me] = msg[me]
    load_c.wait()
    wait_bytes(slotrecv.at[pl.ds(0, n - 1)], slot_recv)
    to_scalars = pltpu.make_async_copy(slotrecv, slot_s, load_sem.at[2])
    to_scalars.start()
    to_scalars.wait()

    @pl.loop(0, CAP)
    def _(j):
        @pl.loop(0, n)
        def _(h):
            slot = jnp.minimum(slot_s[h, 0, j], parents - 1)
            c0send[j, h] = cent[slot]

        c0recv[j, me] = c0send[j, me]

        @pl.loop(1, n)
        def _(i):
            p = peer(i)
            pltpu.make_async_remote_copy(
                src_ref=c0send.at[j, p], dst_ref=c0recv.at[j, me],
                send_sem=c0_send.at[j], recv_sem=c0_recv.at[j],
                device_id=(p, g), device_id_type=MESH,
            ).start()

    slots_out[...] = slotrecv[...]

    lane = lax.broadcasted_iota(jnp.int32, (children, LANES), 1)
    first = lane < block
    load_x.wait()

    def rows_of(j, index):
        at = j * chunk + 2 * index
        return jnp.concatenate([x[meta[0, at]], x[meta[0, at + 1]]], axis=0)

    eye = lax.broadcasted_iota(jnp.int32, (LANES, LANES), 0) == lax.broadcasted_iota(
        jnp.int32, (LANES, LANES), 1
    )

    @pl.loop(0, CAP)
    def _(j):
        @pl.loop(0, groups)
        def _(o):
            for q in range(per_owner):
                rows = rows_of(j, o * per_owner + q)
                gram = dot_t(rows, rows)
                rsend[o, pl.ds(j * per_owner + q, 1), :] = jnp.sum(
                    jnp.where(eye, gram, 0.0), axis=0, keepdims=True
                )

    @pl.loop(1, groups)
    def _(i):
        o = mate(i)
        pltpu.make_async_remote_copy(
            src_ref=rsend.at[o], dst_ref=rrecv.at[g],
            send_sem=r_send, recv_sem=r_recv,
            device_id=(me, o), device_id_type=MESH,
        ).start()

    wait_bytes(rrecv.at[pl.ds(0, groups - 1)], r_recv)
    row_sq = rsend[g]
    for i in range(1, groups):
        row_sq += rrecv[mate(i)]
    rscale[...] = lax.rsqrt(row_sq + epsilon)

    def updated(j, t, o, q, rows):
        at = 2 * (o * per_owner + q)
        old = jnp.concatenate([cur[at], cur[at + 1]], axis=0).astype(jnp.float32)
        weights = wbuf[j, t, o, q].astype(jnp.float32)
        both = jnp.concatenate(
            [jnp.where(first, weights, 0.0), jnp.where(first, 0.0, weights)], axis=0
        )
        moments = jnp.dot(both.astype(jnp.bfloat16), rows, preferred_element_type=jnp.float32)
        totals = jnp.sum(both, axis=1, keepdims=True)
        return ((moments + prior * old) * (1.0 / (totals + prior))).astype(jnp.bfloat16)

    def keep(o, q, both):
        at = 2 * (o * per_owner + q)
        cur[at] = both[:children]
        cur[at + 1] = both[children:]

    @pl.loop(0, CAP)
    def _(j):
        wait_bytes(c0recv.at[j, pl.ds(0, n - 1)], c0_recv.at[j])

        @pl.loop(0, n)
        def _(h):
            start[h] = c0recv[j, h]

        for t in range(ITERS):

            def send_scores(i):
                o = mate(i)
                pltpu.make_async_remote_copy(
                    src_ref=ysend.at[j, t, o], dst_ref=yrecv.at[j, t, g],
                    send_sem=y_send.at[j, t], recv_sem=y_recv.at[j, t],
                    device_id=(me, o), device_id_type=MESH,
                ).start()

            @pl.loop(1, groups + 1)
            def _(i):
                @pl.when(i > 1)
                def _():
                    send_scores(i - 1)

                o = mate(i)
                centre_sq = jnp.zeros((children, LANES), jnp.float32)
                for q in range(per_owner):
                    index = o * per_owner + q
                    rows = rows_of(j, index)
                    if t == 0:
                        at = j * chunk + 2 * index
                        both = jnp.concatenate(
                            [start[meta[1, at]], start[meta[1, at + 1]]], axis=0
                        )
                    else:
                        both = updated(j, t - 1, o, q, rows)
                    keep(o, q, both)
                    part = dot_t(both, rows)
                    ysend[j, t, o, q] = jnp.where(first, part[:children], part[children:])
                    wide = both.astype(jnp.float32)
                    sq = jnp.sum(wide * wide, axis=1, keepdims=True)
                    centre_sq = jnp.where(lane == 2 * q, sq[:children], centre_sq)
                    centre_sq = jnp.where(lane == 2 * q + 1, sq[children:], centre_sq)
                ysend[j, t, o, per_owner] = centre_sq

            wait_bytes(yrecv.at[j, t, pl.ds(0, groups - 1)], y_recv.at[j, t])

            def total(q):
                value = ysend[j, t, g, q]
                for i in range(1, groups):
                    value += yrecv[j, t, mate(i), q]
                return value

            centre_scale = lax.rsqrt(total(per_owner) + epsilon)
            for q in range(per_owner):
                at = j * chunk + 2 * (g * per_owner + q)
                centres = jnp.where(
                    first, centre_scale[:, 2 * q : 2 * q + 1], centre_scale[:, 2 * q + 1 : 2 * q + 2]
                )
                scores = (
                    total(q) * centres * rscale[pl.ds(j * per_owner + q, 1), :] * (1.0 / sharpness)
                )
                raised = jnp.exp(scores)
                share = raised * (1.0 / jnp.sum(raised, axis=0, keepdims=True))
                live = lane < jnp.where(first, meta[2, at], meta[2, at + 1] + block)
                wbuf[j, t, g, q] = jnp.where(live, share, 0.0).astype(jnp.bfloat16)

            wait_bytes(ysend.at[j, t, pl.ds(0, groups - 1)], y_send.at[j, t])

            @pl.loop(1, groups)
            def _(i):
                pltpu.make_async_remote_copy(
                    src_ref=wbuf.at[j, t, g], dst_ref=wbuf.at[j, t, g],
                    send_sem=w_send.at[j, t], recv_sem=w_recv.at[j, t],
                    device_id=(me, mate(i)), device_id_type=MESH,
                ).start()

            wait_bytes(wbuf.at[j, t, pl.ds(0, groups - 1)], w_recv.at[j, t])

        @pl.loop(0, groups)
        def _(o):
            for q in range(per_owner):
                keep(o, q, updated(j, ITERS - 1, o, q, rows_of(j, o * per_owner + q)))

        @pl.loop(0, n)
        def _(h):
            osend[j, h] = cur[posmap[j, h]]

        @pl.loop(1, n)
        def _(i):
            p = peer(i)
            pltpu.make_async_remote_copy(
                src_ref=osend.at[j, p], dst_ref=out.at[j, me],
                send_sem=o_send.at[j], recv_sem=o_recv.at[j],
                device_id=(p, g), device_id_type=MESH,
            ).start()

        pltpu.make_async_copy(osend.at[j, me], out.at[j, me], own_sem.at[j]).start()

    wait_bytes(msg.at[pl.ds(0, n - 1)], slot_send)
    wait_bytes(rsend.at[pl.ds(0, groups - 1)], r_send)

    @pl.loop(0, CAP)
    def _(j):
        wait_bytes(c0send.at[j, pl.ds(0, n - 1)], c0_send.at[j])
        for t in range(ITERS):
            wait_bytes(wbuf.at[j, t, pl.ds(0, groups - 1)], w_send.at[j, t])
        wait_bytes(osend.at[j, pl.ds(0, n - 1)], o_send.at[j])
        pltpu.make_async_copy(osend.at[j, me], out.at[j, me], own_sem.at[j]).wait()
        wait_bytes(out.at[j, pl.ds(0, n - 1)], o_recv.at[j])


def on_device(embeddings, lengths, parent_slot, centroids):
    parents, block, width = embeddings.shape
    children = centroids.shape[1]
    n = lax.axis_size("dp")
    groups = lax.axis_size("grp")
    chunk = parents // CAP
    per_owner = chunk // 2 // groups
    stride = 27 if n % 27 else 1

    holder = parent_slot // parents
    local = parent_slot - holder * parents
    ids = jnp.arange(parents, dtype=jnp.int32)
    earlier = ids[None, :] < ids[:, None]
    order = jnp.sum((earlier & (holder[None, :] == holder[:, None])).astype(jnp.int32), axis=1)
    within = jnp.sum((earlier & (order[None, :] == order[:, None])).astype(jnp.int32), axis=1)
    place = order * chunk + within
    at_place = (place[None, :] == ids[:, None]).astype(jnp.int32)
    meta = jnp.sum(at_place[None] * jnp.stack([ids, holder, lengths])[:, None, :], axis=2)
    cells = jnp.arange(CAP * n, dtype=jnp.int32)
    at_cell = ((order * n + holder)[None, :] == cells[:, None]).astype(jnp.int32)
    posmap = jnp.sum(at_cell * within[None, :], axis=1).reshape(CAP, n)
    asked = jnp.sum(at_cell * (local - parents)[None, :], axis=1).reshape(CAP, n) + parents
    msg = jnp.pad(asked.T, ((0, 0), (0, LANES - CAP)))[:, None, :]

    dma = pltpu.SemaphoreType.DMA
    cell_block = (CAP, n, children, width)
    vmem, smem = pltpu.VMEM, pltpu.SMEM
    out, slots = pl.pallas_call(
        functools.partial(kernel, n, groups, stride),
        out_shape=(
            jax.ShapeDtypeStruct(cell_block, jnp.bfloat16),
            jax.ShapeDtypeStruct((n, 1, LANES), jnp.int32),
        ),
        in_specs=[
            pl.BlockSpec(memory_space=vmem),
            pl.BlockSpec(memory_space=smem),
            pl.BlockSpec(memory_space=smem),
            pl.BlockSpec(memory_space=pl.ANY),
            pl.BlockSpec(memory_space=pl.ANY),
        ],
        out_specs=(pl.BlockSpec(memory_space=pl.ANY), pl.BlockSpec(memory_space=vmem)),
        scratch_shapes=[
            vmem((parents, block, width), jnp.bfloat16),
            vmem((parents, children, width), jnp.bfloat16),
            vmem((n, 1, LANES), jnp.int32),
            smem((n, 1, LANES), jnp.int32),
            vmem(cell_block, jnp.bfloat16),
            vmem(cell_block, jnp.bfloat16),
            vmem(cell_block[1:], jnp.bfloat16),
            vmem(cell_block, jnp.bfloat16),
            vmem((chunk, children, width), jnp.bfloat16),
            vmem((CAP, ITERS, groups, per_owner + 1, children, LANES), jnp.float32),
            vmem((CAP, ITERS, groups, per_owner + 1, children, LANES), jnp.float32),
            vmem((CAP, ITERS, groups, per_owner, children, LANES), jnp.bfloat16),
            vmem((groups, CAP * per_owner, LANES), jnp.float32),
            vmem((groups, CAP * per_owner, LANES), jnp.float32),
            vmem((CAP * per_owner, LANES), jnp.float32),
            dma((3,)),
            dma, dma,
            dma((CAP,)), dma((CAP,)), dma((CAP,)), dma((CAP,)), dma((CAP,)),
            dma, dma,
            dma((CAP, ITERS)), dma((CAP, ITERS)), dma((CAP, ITERS)), dma((CAP, ITERS)),
        ],
        compiler_params=pltpu.CompilerParams(collective_id=0, has_side_effects=True),
        name="refine",
    )(msg, meta, posmap, embeddings, centroids)

    asked_here = slots[:, 0, :CAP].T.reshape(1, CAP * n)
    source = jnp.sum(
        (asked_here == ids[:, None]).astype(jnp.int32) * cells[None, :], axis=1
    )
    rows = out.reshape(CAP * n, children, width)
    return rows.at[source].get(mode="promise_in_bounds")


def solution(mesh):
    return jax.shard_map(
        on_device,
        mesh=mesh,
        in_specs=(P("dp", None, "grp"), P("dp"), P("dp"), P("dp", None, "grp")),
        out_specs=P("dp", None, "grp"),
        check_vma=False,
    )
```

```python
import functools

import jax
import jax.numpy as jnp
from jax import lax
from jax.experimental import pallas as pl
from jax.experimental.pallas import tpu as pltpu
from jax.sharding import PartitionSpec as P

ITERS = 2
CAP = 4
LANES = 128

sharpness = 0.02
prior = 1.0
epsilon = 1e-06

MESH = pl.DeviceIdType.MESH


def wait_bytes(ref, sem):
    pltpu.make_async_copy(ref, ref, sem).wait()


def dot_t(left, right):
    return lax.dot_general(
        left, right, (((1,), (1,)), ((), ())), preferred_element_type=jnp.float32
    )


def kernel(
    n, groups, stride,
    slot_hbm, length_hbm, x_hbm, cent_hbm,
    refined,
    slot_v, length_v, msg_flat, msg, meta_v, meta, inverse_v, inverse,
    x, cent, slotrecv, slot_s, c0send, c0recv, start, osend, orecv, cur,
    ysend, yrecv, wbuf, rsend, rrecv, rscale,
    load_sem, slot_send, slot_recv, c0_send, c0_recv, o_send, o_recv,
    r_send, r_recv, y_send, y_recv, w_send, w_recv,
):
    parents, block, width = x.shape
    children = cent.shape[1]
    chunk = parents // CAP
    per_owner = chunk // 2 // groups
    me = lax.axis_index("dp")
    g = lax.axis_index("grp")

    def peer(i):
        return lax.rem(me + lax.rem(i * stride, n), n)

    def mate(i):
        return lax.rem(g + i, groups)

    def load(source, target, k):
        copy = pltpu.make_async_copy(source, target, load_sem.at[k])
        copy.start()
        return copy

    load_slot = load(slot_hbm, slot_v, 0)
    load_length = load(length_hbm, length_v, 1)

    barrier = pltpu.get_barrier_semaphore()

    @pl.loop(1, n)
    def _(i):
        pl.semaphore_signal(barrier, inc=1, device_id=(peer(i), g), device_id_type=MESH)

    @pl.loop(1, groups)
    def _(i):
        pl.semaphore_signal(barrier, inc=1, device_id=(me, mate(i)), device_id_type=MESH)

    load_c = load(cent_hbm, cent, 2)
    load_x = load(x_hbm, x, 3)
    load_slot.wait()
    load_length.wait()

    def iota(shape, dim):
        return lax.broadcasted_iota(jnp.int32, shape, dim)

    square = (parents, parents)
    sub, lan = iota(square, 0), iota(square, 1)

    def column(row):
        return jnp.sum(jnp.where(sub == lan, row, 0), axis=1, keepdims=True)

    def count(mask, axis):
        return jnp.sum(jnp.where(mask, 1, 0), axis=axis, keepdims=True)

    bits = parents.bit_length() - 1
    slot_row = slot_v[...]
    holder_row = lax.shift_right_logical(slot_row, bits)
    local_row = slot_row - lax.shift_left(holder_row, bits)
    holder = column(holder_row)
    same = holder == holder_row
    order_row = count(same & (sub < lan), 0)
    order = count(same & (lan < sub), 1)

    asked = jnp.zeros((n, LANES), jnp.int32)
    for j in range(CAP):
        hit = (holder_row == iota((n, parents), 0)) & (order_row == j)
        slot_j = jnp.sum(jnp.where(hit, local_row - parents, 0), axis=1, keepdims=True) + parents
        asked = jnp.where(iota((n, LANES), 1) == j, slot_j, asked)
    msg_flat[...] = asked

    @pl.loop(0, n)
    def _(h):
        msg[h] = msg_flat[pl.ds(h, 1), :]

    slotrecv[me] = msg[me]

    within = count((order == order_row) & (lan < sub), 1)
    hit = order * chunk + within == lan
    for k, value in enumerate((sub, holder, column(length_v[...]))):
        meta_v[k] = jnp.sum(jnp.where(hit, value, 0), axis=0, keepdims=True)
    for j in range(CAP):
        hit = (holder == lan) & (order == j)
        meta_v[3 + j] = jnp.sum(jnp.where(hit, within, 0), axis=0, keepdims=True)
    to_meta = load(meta_v, meta, 4)

    pl.semaphore_wait(barrier, n - 1 + groups - 1)

    @pl.loop(1, n)
    def _(i):
        p = peer(i)
        pltpu.make_async_remote_copy(
            src_ref=msg.at[p], dst_ref=slotrecv.at[me],
            send_sem=slot_send, recv_sem=slot_recv,
            device_id=(p, g), device_id_type=MESH,
        ).start()

    load_c.wait()
    to_meta.wait()
    wait_bytes(slotrecv.at[pl.ds(0, n - 1)], slot_recv)
    to_scalars = load(slotrecv, slot_s, 5)
    to_scalars.wait()

    @pl.loop(0, CAP)
    def _(j):
        @pl.loop(0, n, step=4)
        def _(h):
            for k in range(4):
                slot = jnp.minimum(slot_s[h + k, 0, j], parents - 1)
                c0send[j, h + k] = cent[slot]

        c0recv[j, me] = c0send[j, me]

        @pl.loop(1, n)
        def _(i):
            p = peer(i)
            pltpu.make_async_remote_copy(
                src_ref=c0send.at[j, p], dst_ref=c0recv.at[j, me],
                send_sem=c0_send.at[j], recv_sem=c0_recv.at[j],
                device_id=(p, g), device_id_type=MESH,
            ).start()

    row = iota((1, parents), 1)

    def note(s, found):
        for j in range(CAP):
            found = jnp.where(row == slot_s[s, 0, j], j * n + s, found)
        return found

    inverse_v[0] = lax.fori_loop(0, n, note, jnp.zeros((1, parents), jnp.int32))
    to_inverse = load(inverse_v, inverse, 6)

    lane = iota((children, LANES), 1)
    first = lane < block
    load_x.wait()

    def rows_of(j, index):
        at = j * chunk + 2 * index
        return jnp.concatenate([x[meta[0, 0, at]], x[meta[0, 0, at + 1]]], axis=0)

    eye = iota((LANES, LANES), 0) == iota((LANES, LANES), 1)

    @pl.loop(0, CAP)
    def _(j):
        @pl.loop(0, groups)
        def _(o):
            for q in range(per_owner):
                rows = rows_of(j, o * per_owner + q)
                gram = dot_t(rows, rows)
                rsend[o, pl.ds(j * per_owner + q, 1), :] = jnp.sum(
                    jnp.where(eye, gram, 0.0), axis=0, keepdims=True
                )

    @pl.loop(1, groups)
    def _(i):
        o = mate(i)
        pltpu.make_async_remote_copy(
            src_ref=rsend.at[o], dst_ref=rrecv.at[g],
            send_sem=r_send, recv_sem=r_recv,
            device_id=(me, o), device_id_type=MESH,
        ).start()

    to_inverse.wait()
    wait_bytes(rrecv.at[pl.ds(0, groups - 1)], r_recv)
    row_sq = rsend[g]
    for i in range(1, groups):
        row_sq += rrecv[mate(i)]
    rscale[...] = lax.rsqrt(row_sq + epsilon)

    def place(j, o, q):
        return lax.rem(j, 2) * chunk + 2 * (o * per_owner + q)

    def updated(j, t, o, q, rows):
        at = place(j, o, q)
        old = jnp.concatenate([cur[at], cur[at + 1]], axis=0).astype(jnp.float32)
        weights = wbuf[j, t, o, q].astype(jnp.float32)
        both = jnp.concatenate(
            [jnp.where(first, weights, 0.0), jnp.where(first, 0.0, weights)], axis=0
        )
        moments = jnp.dot(both.astype(jnp.bfloat16), rows, preferred_element_type=jnp.float32)
        totals = jnp.sum(both, axis=1, keepdims=True)
        return ((moments + prior * old) * (1.0 / (totals + prior))).astype(jnp.bfloat16)

    def keep(j, o, q, both):
        at = place(j, o, q)
        cur[at] = both[:children]
        cur[at + 1] = both[children:]

    def send_scores(j, t):
        def send(i):
            o = mate(i)
            pltpu.make_async_remote_copy(
                src_ref=ysend.at[j, t, o], dst_ref=yrecv.at[j, t, g],
                send_sem=y_send.at[j, t], recv_sem=y_recv.at[j, t],
                device_id=(me, o), device_id_type=MESH,
            ).start()

        @pl.loop(1, groups + 1)
        def _(i):
            @pl.when(i > 1)
            def _():
                send(i - 1)

            o = mate(i)
            centre_sq = jnp.zeros((children, LANES), jnp.float32)
            for q in range(per_owner):
                index = o * per_owner + q
                rows = rows_of(j, index)
                if t == 0:
                    at = j * chunk + 2 * index
                    both = jnp.concatenate(
                        [start[meta[1, 0, at]], start[meta[1, 0, at + 1]]], axis=0
                    )
                else:
                    both = updated(j, t - 1, o, q, rows)
                keep(j, o, q, both)
                part = dot_t(both, rows)
                ysend[j, t, o, q] = jnp.where(first, part[:children], part[children:])
                wide = both.astype(jnp.float32)
                sq = jnp.sum(wide * wide, axis=1, keepdims=True)
                centre_sq = jnp.where(lane == 2 * q, sq[:children], centre_sq)
                centre_sq = jnp.where(lane == 2 * q + 1, sq[children:], centre_sq)
            ysend[j, t, o, per_owner] = centre_sq

    def begin(j):
        wait_bytes(c0recv.at[j, pl.ds(0, n - 1)], c0_recv.at[j])

        @pl.loop(0, n, step=4)
        def _(h):
            for k in range(4):
                start[h + k] = c0recv[j, h + k]

        send_scores(j, 0)

    def weigh(j, t):
        wait_bytes(yrecv.at[j, t, pl.ds(0, groups - 1)], y_recv.at[j, t])

        def total(q):
            value = ysend[j, t, g, q]
            for i in range(1, groups):
                value += yrecv[j, t, mate(i), q]
            return value

        centre_scale = lax.rsqrt(total(per_owner) + epsilon)
        for q in range(per_owner):
            at = j * chunk + 2 * (g * per_owner + q)
            centres = jnp.where(
                first, centre_scale[:, 2 * q : 2 * q + 1], centre_scale[:, 2 * q + 1 : 2 * q + 2]
            )
            scores = (
                total(q) * centres * rscale[pl.ds(j * per_owner + q, 1), :] * (1.0 / sharpness)
            )
            raised = jnp.exp(scores)
            share = raised * (1.0 / jnp.sum(raised, axis=0, keepdims=True))
            live = lane < jnp.where(first, meta[2, 0, at], meta[2, 0, at + 1] + block)
            wbuf[j, t, g, q] = jnp.where(live, share, 0.0).astype(jnp.bfloat16)

        wait_bytes(ysend.at[j, t, pl.ds(0, groups - 1)], y_send.at[j, t])

        @pl.loop(1, groups)
        def _(i):
            pltpu.make_async_remote_copy(
                src_ref=wbuf.at[j, t, g], dst_ref=wbuf.at[j, t, g],
                send_sem=w_send.at[j, t], recv_sem=w_recv.at[j, t],
                device_id=(me, mate(i)), device_id_type=MESH,
            ).start()

    def weights_here(j, t):
        wait_bytes(wbuf.at[j, t, pl.ds(0, groups - 1)], w_recv.at[j, t])

    def step_again(j):
        weights_here(j, 0)
        send_scores(j, 1)

    def finish(j):
        weights_here(j, ITERS - 1)

        @pl.loop(0, groups)
        def _(o):
            for q in range(per_owner):
                keep(j, o, q, updated(j, ITERS - 1, o, q, rows_of(j, o * per_owner + q)))

        base = lax.rem(j, 2) * chunk

        @pl.loop(0, n, step=4)
        def _(h):
            for k in range(4):
                osend[j, h + k] = cur[base + meta[3 + j, 0, h + k]]

        orecv[j * n + me] = osend[j, me]

        @pl.loop(1, n)
        def _(i):
            p = peer(i)
            pltpu.make_async_remote_copy(
                src_ref=osend.at[j, p], dst_ref=orecv.at[j * n + me],
                send_sem=o_send.at[j], recv_sem=o_recv.at[j],
                device_id=(p, g), device_id_type=MESH,
            ).start()

    begin(0)
    weigh(0, 0)
    step_again(0)

    @pl.loop(1, CAP)
    def _(j):
        begin(j)
        weigh(j - 1, 1)
        weigh(j, 0)
        finish(j - 1)
        step_again(j)

    weigh(CAP - 1, 1)
    finish(CAP - 1)

    wait_bytes(msg.at[pl.ds(0, n - 1)], slot_send)
    wait_bytes(rsend.at[pl.ds(0, groups - 1)], r_send)

    @pl.loop(0, CAP)
    def _(j):
        wait_bytes(c0send.at[j, pl.ds(0, n - 1)], c0_send.at[j])
        for t in range(ITERS):
            wait_bytes(wbuf.at[j, t, pl.ds(0, groups - 1)], w_send.at[j, t])
        wait_bytes(osend.at[j, pl.ds(0, n - 1)], o_send.at[j])
        wait_bytes(orecv.at[pl.ds(0, n - 1)], o_recv.at[j])

    @pl.loop(0, parents, step=8)
    def _(l):
        for k in range(8):
            refined[l + k] = orecv[inverse[0, 0, l + k]]


def on_device(embeddings, lengths, parent_slot, centroids):
    parents, block, width = embeddings.shape
    children = centroids.shape[1]
    n = lax.axis_size("dp")
    groups = lax.axis_size("grp")
    chunk = parents // CAP
    per_owner = chunk // 2 // groups
    stride = 27 if n % 27 else 1

    dma = pltpu.SemaphoreType.DMA
    vmem, smem = pltpu.VMEM, pltpu.SMEM
    cells = (CAP, n, children, width)
    ints = (n, 1, LANES)
    bf16, f32, i32 = jnp.bfloat16, jnp.float32, jnp.int32
    by_owner = (CAP, ITERS, groups, per_owner + 1, children, LANES)
    return pl.pallas_call(
        functools.partial(kernel, n, groups, stride),
        out_shape=jax.ShapeDtypeStruct(centroids.shape, bf16),
        in_specs=[pl.BlockSpec(memory_space=pl.ANY)] * 4,
        out_specs=pl.BlockSpec(memory_space=vmem),
        scratch_shapes=[
            vmem((1, parents), i32),
            vmem((1, parents), i32),
            vmem((n, LANES), i32),
            vmem(ints, i32),
            vmem((3 + CAP, 1, parents), i32),
            smem((3 + CAP, 1, parents), i32),
            vmem((1, 1, parents), i32),
            smem((1, 1, parents), i32),
            vmem((parents, block, width), bf16),
            vmem((parents, children, width), bf16),
            vmem(ints, i32),
            smem(ints, i32),
            vmem(cells, bf16),
            vmem(cells, bf16),
            vmem(cells[1:], bf16),
            vmem(cells, bf16),
            vmem((CAP * n, children, width), bf16),
            vmem((2 * chunk, children, width), bf16),
            vmem(by_owner, f32),
            vmem(by_owner, f32),
            vmem((CAP, ITERS, groups, per_owner, children, LANES), bf16),
            vmem((groups, CAP * per_owner, LANES), f32),
            vmem((groups, CAP * per_owner, LANES), f32),
            vmem((CAP * per_owner, LANES), f32),
            dma((7,)),
            dma, dma,
            dma((CAP,)), dma((CAP,)), dma((CAP,)), dma((CAP,)),
            dma, dma,
            dma((CAP, ITERS)), dma((CAP, ITERS)), dma((CAP, ITERS)), dma((CAP, ITERS)),
        ],
        compiler_params=pltpu.CompilerParams(collective_id=0, has_side_effects=True),
        name="refine",
    )(parent_slot.reshape(1, parents), lengths.reshape(1, parents), embeddings, centroids)


def solution(mesh):
    return jax.shard_map(
        on_device,
        mesh=mesh,
        in_specs=(P("dp", None, "grp"), P("dp"), P("dp"), P("dp", None, "grp")),
        out_specs=P("dp", None, "grp"),
        check_vma=False,
    )
```

```python
import functools

import jax
import jax.numpy as jnp
from jax import lax
from jax.experimental import pallas as pl
from jax.experimental.pallas import tpu as pltpu
from jax.sharding import PartitionSpec as P

ITERS = 2
CAP = 4
LANES = 128

sharpness = 0.02
prior = 1.0
epsilon = 1e-06

MESH = pl.DeviceIdType.MESH


def wait_bytes(ref, sem):
    pltpu.make_async_copy(ref, ref, sem).wait()


def dot_t(left, right):
    return lax.dot_general(
        left, right, (((1,), (1,)), ((), ())), preferred_element_type=jnp.float32
    )


def kernel(
    n, groups, shape,
    slot_hbm, length_hbm, x_hbm, cent_hbm,
    refined,
    slot_v, length_v, msg_flat, msg, meta_v, meta, inverse_v, inverse,
    x, cent, slotrecv, slot_s, c0send, c0recv, start, osend, orecv, cur,
    ysend, yrecv, wbuf, rsend, rrecv, rscale,
    load_sem, ring_sem, slot_send, slot_recv, c0_send, c0_recv, o_send, o_recv,
    r_send, r_recv, y_send, y_recv, w_send, w_recv,
):
    parents, block, width = x.shape
    children = cent.shape[1]
    chunk = parents // CAP
    per_owner = chunk // 2 // groups
    me = lax.axis_index("dp")
    g = lax.axis_index("grp")

    lines, planes, cores = shape
    side = lines * cores
    my_core = lax.rem(me, cores)
    my_plane = lax.rem(lax.div(me, cores), planes)
    my_line = lax.div(me, cores * planes)

    def peer(away, k):
        line = lax.rem(my_line + lax.div(k, cores), lines)
        plane = lax.rem(my_plane + away, planes)
        core = lax.rem(my_core + lax.rem(k, cores), cores)
        return (line * planes + plane) * cores + core

    def each(distance, act):
        def call(away, k, here, there):
            line = lax.rem(lines - lax.div(k, cores), lines)
            core = lax.rem(cores - lax.rem(k, cores), cores)
            act(peer(away, k), here * side + k, there * side + line * cores + core)

        if distance == 0:
            pl.loop(1, side)(lambda k: call(0, k, 0, 0))
        elif 2 * distance == planes:
            pl.loop(0, side)(lambda k: call(distance, k, planes - 1, planes - 1))
        else:

            @pl.loop(0, 2 * side)
            def _(i):
                turn = lax.rem(i, 2)
                low = 2 * distance - 1
                call(distance + turn * (planes - 2 * distance), lax.div(i, 2), low + turn, low + 1 - turn)

    reach = planes // 2
    near_rows = 3 * side

    def near(act):
        each(1, act)
        each(0, act)

    def far(act):
        for distance in range(reach, 1, -1):
            each(distance, act)

    def everyone(act):
        far(act)
        near(act)

    def mate(i):
        return lax.rem(g + i, groups)

    def load(source, target, k):
        copy = pltpu.make_async_copy(source, target, load_sem.at[k])
        copy.start()
        return copy

    load_slot = load(slot_hbm, slot_v, 0)
    load_length = load(length_hbm, length_v, 1)

    barrier = pltpu.get_barrier_semaphore()

    @near
    def _(p, here, there):
        pl.semaphore_signal(barrier, inc=1, device_id=(p, g), device_id_type=MESH)

    @pl.loop(1, groups)
    def _(i):
        pl.semaphore_signal(barrier, inc=1, device_id=(me, mate(i)), device_id_type=MESH)

    load_c = load(cent_hbm, cent, 2)
    load_x = load(x_hbm, x, 3)
    load_slot.wait()
    load_length.wait()

    def iota(shape, dim):
        return lax.broadcasted_iota(jnp.int32, shape, dim)

    square = (parents, parents)
    sub, lan = iota(square, 0), iota(square, 1)

    def column(row):
        return jnp.sum(jnp.where(sub == lan, row, 0), axis=1, keepdims=True)

    def count(mask, axis):
        return jnp.sum(jnp.where(mask, 1, 0), axis=axis, keepdims=True)

    bits = parents.bit_length() - 1
    slot_row = slot_v[...]
    holder_row = lax.shift_right_logical(slot_row, bits)
    local_row = slot_row - lax.shift_left(holder_row, bits)
    holder = column(holder_row)
    same = holder == holder_row
    order_row = count(same & (sub < lan), 0)
    order = count(same & (lan < sub), 1)

    asked = jnp.zeros((n, LANES), jnp.int32)
    for j in range(CAP):
        hit = (holder_row == iota((n, parents), 0)) & (order_row == j)
        slot_j = jnp.sum(jnp.where(hit, local_row - parents, 0), axis=1, keepdims=True) + parents
        asked = jnp.where(iota((n, LANES), 1) == j, slot_j, asked)
    msg_flat[...] = asked

    @pl.loop(0, n)
    def _(h):
        msg[h] = msg_flat[pl.ds(h, 1), :]

    slotrecv[0] = msg[me]
    pl.semaphore_wait(barrier, near_rows - 1 + groups - 1)

    def ask(k):
        def send(p, here, there):
            pltpu.make_async_remote_copy(
                src_ref=msg.at[p], dst_ref=slotrecv.at[there],
                send_sem=slot_send, recv_sem=slot_recv.at[k],
                device_id=(p, g), device_id_type=MESH,
            ).start()

        return send

    near(ask(0))
    for distance in range(2, reach + 1):
        ring = ring_sem.at[distance - 2]
        for away in (1, planes - 1):
            pl.semaphore_signal(ring, inc=1, device_id=(peer(away, 0), g), device_id_type=MESH)
        pl.semaphore_wait(ring, 2)
        each(distance, ask(1))

    def serve(j, who):
        @who
        def _(p, here, there):
            c0send[j, p] = cent[jnp.minimum(slot_s[here, 0, j], parents - 1)]

        @who
        def _(p, here, there):
            pltpu.make_async_remote_copy(
                src_ref=c0send.at[j, p], dst_ref=c0recv.at[j, me],
                send_sem=c0_send.at[j], recv_sem=c0_recv.at[j],
                device_id=(p, g), device_id_type=MESH,
            ).start()

    def to_scalars(first_row, rows, k):
        part = pl.ds(first_row, rows)
        load(slotrecv.at[part], slot_s.at[part], k).wait()

    load_c.wait()
    wait_bytes(slotrecv.at[pl.ds(0, near_rows - 1)], slot_recv.at[0])
    to_scalars(0, near_rows, 5)

    @pl.loop(0, CAP)
    def _(j):
        c0recv[j, me] = cent[jnp.minimum(slot_s[0, 0, j], parents - 1)]
        serve(j, near)

    within = count((order == order_row) & (lan < sub), 1)
    hit = order * chunk + within == lan
    for k, value in enumerate((sub, holder, column(length_v[...]))):
        meta_v[k] = jnp.sum(jnp.where(hit, value, 0), axis=0, keepdims=True)
    for j in range(CAP):
        hit = (holder == lan) & (order == j)
        meta_v[3 + j] = jnp.sum(jnp.where(hit, within, 0), axis=0, keepdims=True)
    to_meta = load(meta_v, meta, 4)


    wait_bytes(slotrecv.at[pl.ds(near_rows, n - near_rows)], slot_recv.at[1])
    to_scalars(near_rows, n - near_rows, 7)

    @pl.loop(0, CAP)
    def _(j):
        serve(j, far)

    to_meta.wait()

    row = iota((1, parents), 1)

    def note(p, here, there):
        found = inverse_v[0]
        for j in range(CAP):
            found = jnp.where(row == slot_s[here, 0, j], j * n + p, found)
        inverse_v[0] = found

    inverse_v[0] = jnp.zeros((1, parents), jnp.int32)
    note(me, 0, 0)
    everyone(note)
    to_inverse = load(inverse_v, inverse, 6)

    lane = iota((children, LANES), 1)
    first = lane < block
    load_x.wait()

    def rows_of(j, index):
        at = j * chunk + 2 * index
        return jnp.concatenate([x[meta[0, 0, at]], x[meta[0, 0, at + 1]]], axis=0)

    eye = iota((LANES, LANES), 0) == iota((LANES, LANES), 1)

    @pl.loop(0, CAP)
    def _(j):
        @pl.loop(0, groups)
        def _(o):
            for q in range(per_owner):
                rows = rows_of(j, o * per_owner + q)
                gram = dot_t(rows, rows)
                rsend[o, pl.ds(j * per_owner + q, 1), :] = jnp.sum(
                    jnp.where(eye, gram, 0.0), axis=0, keepdims=True
                )

    @pl.loop(1, groups)
    def _(i):
        o = mate(i)
        pltpu.make_async_remote_copy(
            src_ref=rsend.at[o], dst_ref=rrecv.at[g],
            send_sem=r_send, recv_sem=r_recv,
            device_id=(me, o), device_id_type=MESH,
        ).start()

    to_inverse.wait()
    wait_bytes(rrecv.at[pl.ds(0, groups - 1)], r_recv)
    row_sq = rsend[g]
    for i in range(1, groups):
        row_sq += rrecv[mate(i)]
    rscale[...] = lax.rsqrt(row_sq + epsilon)

    def place(j, o, q):
        return lax.rem(j, 2) * chunk + 2 * (o * per_owner + q)

    def updated(j, t, o, q, rows):
        at = place(j, o, q)
        old = jnp.concatenate([cur[at], cur[at + 1]], axis=0).astype(jnp.float32)
        weights = wbuf[j, t, o, q].astype(jnp.float32)
        both = jnp.concatenate(
            [jnp.where(first, weights, 0.0), jnp.where(first, 0.0, weights)], axis=0
        )
        moments = jnp.dot(both.astype(jnp.bfloat16), rows, preferred_element_type=jnp.float32)
        totals = jnp.sum(both, axis=1, keepdims=True)
        return ((moments + prior * old) * (1.0 / (totals + prior))).astype(jnp.bfloat16)

    def keep(j, o, q, both):
        at = place(j, o, q)
        cur[at] = both[:children]
        cur[at + 1] = both[children:]

    def send_scores(j, t):
        def send(i):
            o = mate(i)
            pltpu.make_async_remote_copy(
                src_ref=ysend.at[j, t, o], dst_ref=yrecv.at[j, t, g],
                send_sem=y_send.at[j, t], recv_sem=y_recv.at[j, t],
                device_id=(me, o), device_id_type=MESH,
            ).start()

        @pl.loop(1, groups + 1)
        def _(i):
            @pl.when(i > 1)
            def _():
                send(i - 1)

            o = mate(i)
            centre_sq = jnp.zeros((children, LANES), jnp.float32)
            for q in range(per_owner):
                index = o * per_owner + q
                rows = rows_of(j, index)
                if t == 0:
                    at = j * chunk + 2 * index
                    both = jnp.concatenate(
                        [start[meta[1, 0, at]], start[meta[1, 0, at + 1]]], axis=0
                    )
                else:
                    both = updated(j, t - 1, o, q, rows)
                keep(j, o, q, both)
                part = dot_t(both, rows)
                ysend[j, t, o, q] = jnp.where(first, part[:children], part[children:])
                wide = both.astype(jnp.float32)
                sq = jnp.sum(wide * wide, axis=1, keepdims=True)
                centre_sq = jnp.where(lane == 2 * q, sq[:children], centre_sq)
                centre_sq = jnp.where(lane == 2 * q + 1, sq[children:], centre_sq)
            ysend[j, t, o, per_owner] = centre_sq

    def begin(j):
        wait_bytes(c0recv.at[j, pl.ds(0, n - 1)], c0_recv.at[j])

        @pl.loop(0, n, step=4)
        def _(h):
            for k in range(4):
                start[h + k] = c0recv[j, h + k]

        send_scores(j, 0)

    def weigh(j, t):
        wait_bytes(yrecv.at[j, t, pl.ds(0, groups - 1)], y_recv.at[j, t])

        def total(q):
            value = ysend[j, t, g, q]
            for i in range(1, groups):
                value += yrecv[j, t, mate(i), q]
            return value

        centre_scale = lax.rsqrt(total(per_owner) + epsilon)
        for q in range(per_owner):
            at = j * chunk + 2 * (g * per_owner + q)
            centres = jnp.where(
                first, centre_scale[:, 2 * q : 2 * q + 1], centre_scale[:, 2 * q + 1 : 2 * q + 2]
            )
            scores = (
                total(q) * centres * rscale[pl.ds(j * per_owner + q, 1), :] * (1.0 / sharpness)
            )
            raised = jnp.exp(scores)
            share = raised * (1.0 / jnp.sum(raised, axis=0, keepdims=True))
            live = lane < jnp.where(first, meta[2, 0, at], meta[2, 0, at + 1] + block)
            wbuf[j, t, g, q] = jnp.where(live, share, 0.0).astype(jnp.bfloat16)

        wait_bytes(ysend.at[j, t, pl.ds(0, groups - 1)], y_send.at[j, t])

        @pl.loop(1, groups)
        def _(i):
            pltpu.make_async_remote_copy(
                src_ref=wbuf.at[j, t, g], dst_ref=wbuf.at[j, t, g],
                send_sem=w_send.at[j, t], recv_sem=w_recv.at[j, t],
                device_id=(me, mate(i)), device_id_type=MESH,
            ).start()

    def weights_here(j, t):
        wait_bytes(wbuf.at[j, t, pl.ds(0, groups - 1)], w_recv.at[j, t])

    def step_again(j):
        weights_here(j, 0)
        send_scores(j, 1)

    def finish(j):
        weights_here(j, ITERS - 1)

        @pl.loop(0, groups)
        def _(o):
            for q in range(per_owner):
                keep(j, o, q, updated(j, ITERS - 1, o, q, rows_of(j, o * per_owner + q)))

        base = lax.rem(j, 2) * chunk

        @pl.loop(0, n, step=4)
        def _(h):
            for k in range(4):
                osend[j, h + k] = cur[base + meta[3 + j, 0, h + k]]

        orecv[j * n + me] = osend[j, me]

        @everyone
        def _(p, here, there):
            pltpu.make_async_remote_copy(
                src_ref=osend.at[j, p], dst_ref=orecv.at[j * n + me],
                send_sem=o_send.at[j], recv_sem=o_recv.at[j],
                device_id=(p, g), device_id_type=MESH,
            ).start()

    begin(0)
    weigh(0, 0)
    step_again(0)

    @pl.loop(1, CAP)
    def _(j):
        begin(j)
        weigh(j - 1, 1)
        weigh(j, 0)
        finish(j - 1)
        step_again(j)

    weigh(CAP - 1, 1)
    finish(CAP - 1)

    wait_bytes(msg.at[pl.ds(0, n - 1)], slot_send)
    wait_bytes(rsend.at[pl.ds(0, groups - 1)], r_send)

    @pl.loop(0, CAP)
    def _(j):
        wait_bytes(c0send.at[j, pl.ds(0, n - 1)], c0_send.at[j])
        for t in range(ITERS):
            wait_bytes(wbuf.at[j, t, pl.ds(0, groups - 1)], w_send.at[j, t])
        wait_bytes(osend.at[j, pl.ds(0, n - 1)], o_send.at[j])
        wait_bytes(orecv.at[pl.ds(0, n - 1)], o_recv.at[j])

    @pl.loop(0, parents, step=8)
    def _(l):
        for k in range(8):
            refined[l + k] = orecv[inverse[0, 0, l + k]]


def on_device(embeddings, lengths, parent_slot, centroids):
    parents, block, width = embeddings.shape
    children = centroids.shape[1]
    n = lax.axis_size("dp")
    groups = lax.axis_size("grp")
    chunk = parents // CAP
    per_owner = chunk // 2 // groups
    shape = (4, 8, 2) if n == 64 else (1, n // 2, 2)

    dma = pltpu.SemaphoreType.DMA
    vmem, smem = pltpu.VMEM, pltpu.SMEM
    cells = (CAP, n, children, width)
    ints = (n, 1, LANES)
    bf16, f32, i32 = jnp.bfloat16, jnp.float32, jnp.int32
    by_owner = (CAP, ITERS, groups, per_owner + 1, children, LANES)
    return pl.pallas_call(
        functools.partial(kernel, n, groups, shape),
        out_shape=jax.ShapeDtypeStruct(centroids.shape, bf16),
        in_specs=[pl.BlockSpec(memory_space=pl.ANY)] * 4,
        out_specs=pl.BlockSpec(memory_space=vmem),
        scratch_shapes=[
            vmem((1, parents), i32),
            vmem((1, parents), i32),
            vmem((n, LANES), i32),
            vmem(ints, i32),
            vmem((3 + CAP, 1, parents), i32),
            smem((3 + CAP, 1, parents), i32),
            vmem((1, 1, parents), i32),
            smem((1, 1, parents), i32),
            vmem((parents, block, width), bf16),
            vmem((parents, children, width), bf16),
            vmem(ints, i32),
            smem(ints, i32),
            vmem(cells, bf16),
            vmem(cells, bf16),
            vmem(cells[1:], bf16),
            vmem(cells, bf16),
            vmem((CAP * n, children, width), bf16),
            vmem((2 * chunk, children, width), bf16),
            vmem(by_owner, f32),
            vmem(by_owner, f32),
            vmem((CAP, ITERS, groups, per_owner, children, LANES), bf16),
            vmem((groups, CAP * per_owner, LANES), f32),
            vmem((groups, CAP * per_owner, LANES), f32),
            vmem((CAP * per_owner, LANES), f32),
            dma((8,)),
            pltpu.SemaphoreType.REGULAR((shape[1] // 2 - 1,)),
            dma, dma((2,)),
            dma((CAP,)), dma((CAP,)), dma((CAP,)), dma((CAP,)),
            dma, dma,
            dma((CAP, ITERS)), dma((CAP, ITERS)), dma((CAP, ITERS)), dma((CAP, ITERS)),
        ],
        compiler_params=pltpu.CompilerParams(
            collective_id=0, has_side_effects=True, vmem_limit_bytes=28 << 20
        ),
        name="refine",
    )(
        *(
            pltpu.with_memory_space_constraint(value, pltpu.HBM)
            for value in (
                parent_slot.reshape(1, parents),
                lengths.reshape(1, parents),
                embeddings,
                centroids,
            )
        )
    )


def solution(mesh):
    return jax.shard_map(
        on_device,
        mesh=mesh,
        in_specs=(P("dp", None, "grp"), P("dp"), P("dp"), P("dp", None, "grp")),
        out_specs=P("dp", None, "grp"),
        check_vma=False,
    )
```

```python
import functools

import jax
import jax.numpy as jnp
from jax import lax
from jax.experimental import pallas as pl
from jax.experimental.pallas import tpu as pltpu
from jax.sharding import PartitionSpec as P

ITERS = 2
CAP = 4
LANES = 128

sharpness = 0.02
prior = 1.0
epsilon = 1e-06

MESH = pl.DeviceIdType.MESH


def wait_bytes(ref, sem):
    pltpu.make_async_copy(ref, ref, sem).wait()


def dot_t(left, right):
    return lax.dot_general(
        left, right, (((1,), (1,)), ((), ())), preferred_element_type=jnp.float32
    )


def kernel(
    n, groups, shape,
    slot_hbm, length_hbm, x_hbm, cent_hbm,
    refined,
    slot_v, length_v, msg_flat, msg, meta_v, meta, inverse_v, inverse,
    x, cent, slotrecv, slot_s, c0send, c0recv, start, osend, orecv, cur,
    ysend, yrecv, wbuf, rsend, rrecv, rscale,
    load_sem, ring_sem, slot_send, slot_recv, c0_send, c0_recv, o_send, o_recv,
    r_send, r_recv, y_send, y_recv, w_send, w_recv,
):
    parents, block, width = x.shape
    children = cent.shape[1]
    chunk = parents // CAP
    per_owner = chunk // 2 // groups
    me = lax.axis_index("dp")
    g = lax.axis_index("grp")

    lines, planes, cores = shape
    side = lines * cores
    my_core = lax.rem(me, cores)
    my_plane = lax.rem(lax.div(me, cores), planes)
    my_line = lax.div(me, cores * planes)

    def peer(away, k):
        line = lax.rem(my_line + lax.div(k, cores), lines)
        plane = lax.rem(my_plane + away, planes)
        core = lax.rem(my_core + lax.rem(k, cores), cores)
        return (line * planes + plane) * cores + core

    def each(distance, act):
        def call(away, k, here, there):
            line = lax.rem(lines - lax.div(k, cores), lines)
            core = lax.rem(cores - lax.rem(k, cores), cores)
            act(peer(away, k), here * side + k, there * side + line * cores + core)

        if distance == 0:
            pl.loop(1, side)(lambda k: call(0, k, 0, 0))
        elif 2 * distance == planes:
            pl.loop(0, side)(lambda k: call(distance, k, planes - 1, planes - 1))
        else:

            @pl.loop(0, 2 * side)
            def _(i):
                turn = lax.rem(i, 2)
                low = 2 * distance - 1
                call(distance + turn * (planes - 2 * distance), lax.div(i, 2), low + turn, low + 1 - turn)

    reach = planes // 2
    near_rows = 3 * side

    def near(act):
        each(1, act)
        each(0, act)

    def far(act):
        for distance in range(reach, 1, -1):
            each(distance, act)

    def everyone(act):
        far(act)
        near(act)

    def mixed(act):
        @pl.loop(1, n)
        def _(i):
            m = lax.rem(i, planes)
            odd = lax.rem(m, 2)
            half = lax.div(m + 1, 2)
            act(peer(lax.rem(odd * half + (1 - odd) * (planes - half), planes), lax.div(i, planes)), 0, 0)

    def far_mixed(act):
        @pl.loop(0, side * (planes - 3))
        def _(i):
            act(peer(2 + lax.rem(i, planes - 3), lax.div(i, planes - 3)), row_of(2 + lax.rem(i, planes - 3), lax.div(i, planes - 3)), 0)

    def row_of(away, k):
        low = 2 * away - 1
        high = 2 * (planes - away)
        return lax.min(low, high) * side + k

    def mate(i):
        return lax.rem(g + i, groups)

    def load(source, target, k):
        copy = pltpu.make_async_copy(source, target, load_sem.at[k])
        copy.start()
        return copy

    load_slot = load(slot_hbm, slot_v, 0)
    load_length = load(length_hbm, length_v, 1)

    barrier = pltpu.get_barrier_semaphore()

    @near
    def _(p, here, there):
        pl.semaphore_signal(barrier, inc=1, device_id=(p, g), device_id_type=MESH)

    @pl.loop(1, groups)
    def _(i):
        pl.semaphore_signal(barrier, inc=1, device_id=(me, mate(i)), device_id_type=MESH)

    load_c = load(cent_hbm, cent, 2)
    load_x = load(x_hbm, x, 3)
    load_slot.wait()
    load_length.wait()

    def iota(shape, dim):
        return lax.broadcasted_iota(jnp.int32, shape, dim)

    square = (parents, parents)
    sub, lan = iota(square, 0), iota(square, 1)

    def column(row):
        return jnp.sum(jnp.where(sub == lan, row, 0), axis=1, keepdims=True)

    def count(mask, axis):
        return jnp.sum(jnp.where(mask, 1, 0), axis=axis, keepdims=True)

    bits = parents.bit_length() - 1
    slot_row = slot_v[...]
    holder_row = lax.shift_right_logical(slot_row, bits)
    local_row = slot_row - lax.shift_left(holder_row, bits)
    holder = column(holder_row)
    same = holder == holder_row
    order_row = count(same & (sub < lan), 0)
    order = count(same & (lan < sub), 1)

    asked = jnp.zeros((n, LANES), jnp.int32)
    for j in range(CAP):
        hit = (holder_row == iota((n, parents), 0)) & (order_row == j)
        slot_j = jnp.sum(jnp.where(hit, local_row - parents, 0), axis=1, keepdims=True) + parents
        asked = jnp.where(iota((n, LANES), 1) == j, slot_j, asked)
    msg_flat[...] = asked

    @pl.loop(0, n)
    def _(h):
        msg[h] = msg_flat[pl.ds(h, 1), :]

    slotrecv[0] = msg[me]
    pl.semaphore_wait(barrier, near_rows - 1 + groups - 1)

    def ask(k):
        def send(p, here, there):
            pltpu.make_async_remote_copy(
                src_ref=msg.at[p], dst_ref=slotrecv.at[there],
                send_sem=slot_send, recv_sem=slot_recv.at[k],
                device_id=(p, g), device_id_type=MESH,
            ).start()

        return send

    def tell(distance):
        for away in (1, planes - 1):
            pl.semaphore_signal(
                ring_sem.at[distance - 2], inc=1,
                device_id=(peer(away, 0), g), device_id_type=MESH,
            )

    tell(2)
    near(ask(0))
    for distance in range(2, reach + 1):
        pl.semaphore_wait(ring_sem.at[distance - 2], 2)
        if distance < reach:
            tell(distance + 1)
        each(distance, ask(distance - 1))

    def serve(j, who):
        @who
        def _(p, here, there):
            c0send[j, p] = cent[jnp.minimum(slot_s[here, 0, j], parents - 1)]

        @who
        def _(p, here, there):
            pltpu.make_async_remote_copy(
                src_ref=c0send.at[j, p], dst_ref=c0recv.at[j, me],
                send_sem=c0_send.at[j], recv_sem=c0_recv.at[j],
                device_id=(p, g), device_id_type=MESH,
            ).start()

    def to_scalars(first_row, rows, k):
        part = pl.ds(first_row, rows)
        load(slotrecv.at[part], slot_s.at[part], k).wait()

    load_c.wait()
    wait_bytes(slotrecv.at[pl.ds(0, near_rows - 1)], slot_recv.at[0])
    to_scalars(0, near_rows, 5)

    @pl.loop(0, CAP)
    def _(j):
        c0recv[j, me] = cent[jnp.minimum(slot_s[0, 0, j], parents - 1)]
        serve(j, near)

    for distance in range(2, reach + 1):
        first_row = (2 * distance - 1) * side
        rows = side if 2 * distance == planes else 2 * side
        wait_bytes(slotrecv.at[pl.ds(first_row, rows)], slot_recv.at[distance - 1])
        to_scalars(first_row, rows, 5 + distance)
        serve(0, functools.partial(each, distance))

    @pl.loop(1, CAP)
    def _(j):
        serve(j, far_mixed)

    within = count((order == order_row) & (lan < sub), 1)
    hit = order * chunk + within == lan
    for k, value in enumerate((sub, holder, column(length_v[...]))):
        meta_v[k] = jnp.sum(jnp.where(hit, value, 0), axis=0, keepdims=True)
    for j in range(CAP):
        hit = (holder == lan) & (order == j)
        meta_v[3 + j] = jnp.sum(jnp.where(hit, within, 0), axis=0, keepdims=True)
    to_meta = load(meta_v, meta, 4)

    row = iota((1, parents), 1)

    def note(p, here, there):
        found = inverse_v[0]
        for j in range(CAP):
            found = jnp.where(row == slot_s[here, 0, j], j * n + p, found)
        inverse_v[0] = found

    inverse_v[0] = jnp.zeros((1, parents), jnp.int32)
    note(me, 0, 0)
    everyone(note)
    to_inverse = load(inverse_v, inverse, 6)
    to_meta.wait()

    lane = iota((children, LANES), 1)
    first = lane < block
    load_x.wait()

    def rows_of(j, index):
        at = j * chunk + 2 * index
        return jnp.concatenate([x[meta[0, 0, at]], x[meta[0, 0, at + 1]]], axis=0)

    eye = iota((LANES, LANES), 0) == iota((LANES, LANES), 1)

    @pl.loop(0, CAP)
    def _(j):
        @pl.loop(0, groups)
        def _(o):
            for q in range(per_owner):
                rows = rows_of(j, o * per_owner + q)
                gram = dot_t(rows, rows)
                rsend[o, pl.ds(j * per_owner + q, 1), :] = jnp.sum(
                    jnp.where(eye, gram, 0.0), axis=0, keepdims=True
                )

    @pl.loop(1, groups)
    def _(i):
        o = mate(i)
        pltpu.make_async_remote_copy(
            src_ref=rsend.at[o], dst_ref=rrecv.at[g],
            send_sem=r_send, recv_sem=r_recv,
            device_id=(me, o), device_id_type=MESH,
        ).start()

    to_inverse.wait()
    wait_bytes(rrecv.at[pl.ds(0, groups - 1)], r_recv)
    row_sq = rsend[g]
    for i in range(1, groups):
        row_sq += rrecv[mate(i)]
    rscale[...] = lax.rsqrt(row_sq + epsilon)

    def place(j, o, q):
        return lax.rem(j, 2) * chunk + 2 * (o * per_owner + q)

    def updated(j, t, o, q, rows):
        at = place(j, o, q)
        old = jnp.concatenate([cur[at], cur[at + 1]], axis=0).astype(jnp.float32)
        weights = wbuf[j, t, o, q].astype(jnp.float32)
        both = jnp.concatenate(
            [jnp.where(first, weights, 0.0), jnp.where(first, 0.0, weights)], axis=0
        )
        moments = jnp.dot(both.astype(jnp.bfloat16), rows, preferred_element_type=jnp.float32)
        totals = jnp.sum(both, axis=1, keepdims=True)
        return ((moments + prior * old) * (1.0 / (totals + prior))).astype(jnp.bfloat16)

    def keep(j, o, q, both):
        at = place(j, o, q)
        cur[at] = both[:children]
        cur[at + 1] = both[children:]

    def send_scores(j, t):
        def send(i):
            o = mate(i)
            pltpu.make_async_remote_copy(
                src_ref=ysend.at[j, t, o], dst_ref=yrecv.at[j, t, g],
                send_sem=y_send.at[j, t], recv_sem=y_recv.at[j, t],
                device_id=(me, o), device_id_type=MESH,
            ).start()

        @pl.loop(1, groups + 1)
        def _(i):
            @pl.when(i > 1)
            def _():
                send(i - 1)

            o = mate(i)
            centre_sq = jnp.zeros((children, LANES), jnp.float32)
            for q in range(per_owner):
                index = o * per_owner + q
                rows = rows_of(j, index)
                if t == 0:
                    at = j * chunk + 2 * index
                    both = jnp.concatenate(
                        [start[meta[1, 0, at]], start[meta[1, 0, at + 1]]], axis=0
                    )
                else:
                    both = updated(j, t - 1, o, q, rows)
                keep(j, o, q, both)
                part = dot_t(both, rows)
                ysend[j, t, o, q] = jnp.where(first, part[:children], part[children:])
                wide = both.astype(jnp.float32)
                sq = jnp.sum(wide * wide, axis=1, keepdims=True)
                centre_sq = jnp.where(lane == 2 * q, sq[:children], centre_sq)
                centre_sq = jnp.where(lane == 2 * q + 1, sq[children:], centre_sq)
            ysend[j, t, o, per_owner] = centre_sq

    def begin(j):
        wait_bytes(c0recv.at[j, pl.ds(0, n - 1)], c0_recv.at[j])

        @pl.loop(0, n, step=4)
        def _(h):
            for k in range(4):
                start[h + k] = c0recv[j, h + k]

        send_scores(j, 0)

    def weigh(j, t):
        wait_bytes(yrecv.at[j, t, pl.ds(0, groups - 1)], y_recv.at[j, t])

        def total(q):
            value = ysend[j, t, g, q]
            for i in range(1, groups):
                value += yrecv[j, t, mate(i), q]
            return value

        centre_scale = lax.rsqrt(total(per_owner) + epsilon)
        for q in range(per_owner):
            at = j * chunk + 2 * (g * per_owner + q)
            centres = jnp.where(
                first, centre_scale[:, 2 * q : 2 * q + 1], centre_scale[:, 2 * q + 1 : 2 * q + 2]
            )
            scores = (
                total(q) * centres * rscale[pl.ds(j * per_owner + q, 1), :] * (1.0 / sharpness)
            )
            raised = jnp.exp(scores)
            share = raised * (1.0 / jnp.sum(raised, axis=0, keepdims=True))
            live = lane < jnp.where(first, meta[2, 0, at], meta[2, 0, at + 1] + block)
            wbuf[j, t, g, q] = jnp.where(live, share, 0.0).astype(jnp.bfloat16)

        wait_bytes(ysend.at[j, t, pl.ds(0, groups - 1)], y_send.at[j, t])

        @pl.loop(1, groups)
        def _(i):
            pltpu.make_async_remote_copy(
                src_ref=wbuf.at[j, t, g], dst_ref=wbuf.at[j, t, g],
                send_sem=w_send.at[j, t], recv_sem=w_recv.at[j, t],
                device_id=(me, mate(i)), device_id_type=MESH,
            ).start()

    def weights_here(j, t):
        wait_bytes(wbuf.at[j, t, pl.ds(0, groups - 1)], w_recv.at[j, t])

    def step_again(j):
        weights_here(j, 0)
        send_scores(j, 1)

    def finish(j):
        weights_here(j, ITERS - 1)

        @pl.loop(0, groups)
        def _(o):
            for q in range(per_owner):
                keep(j, o, q, updated(j, ITERS - 1, o, q, rows_of(j, o * per_owner + q)))

        base = lax.rem(j, 2) * chunk

        @pl.loop(0, n, step=4)
        def _(h):
            for k in range(4):
                osend[j, h + k] = cur[base + meta[3 + j, 0, h + k]]

        orecv[j * n + me] = osend[j, me]

        @mixed
        def _(p, here, there):
            pltpu.make_async_remote_copy(
                src_ref=osend.at[j, p], dst_ref=orecv.at[j * n + me],
                send_sem=o_send.at[j], recv_sem=o_recv.at[j],
                device_id=(p, g), device_id_type=MESH,
            ).start()

    begin(0)
    weigh(0, 0)
    step_again(0)

    @pl.loop(1, CAP)
    def _(j):
        begin(j)
        weigh(j - 1, 1)
        weigh(j, 0)
        finish(j - 1)
        step_again(j)

    weigh(CAP - 1, 1)
    finish(CAP - 1)

    wait_bytes(msg.at[pl.ds(0, n - 1)], slot_send)
    wait_bytes(rsend.at[pl.ds(0, groups - 1)], r_send)

    @pl.loop(0, CAP)
    def _(j):
        wait_bytes(c0send.at[j, pl.ds(0, n - 1)], c0_send.at[j])
        for t in range(ITERS):
            wait_bytes(wbuf.at[j, t, pl.ds(0, groups - 1)], w_send.at[j, t])
        wait_bytes(osend.at[j, pl.ds(0, n - 1)], o_send.at[j])
        wait_bytes(orecv.at[pl.ds(0, n - 1)], o_recv.at[j])

    @pl.loop(0, parents, step=8)
    def _(l):
        for k in range(8):
            refined[l + k] = orecv[inverse[0, 0, l + k]]


def on_device(embeddings, lengths, parent_slot, centroids):
    parents, block, width = embeddings.shape
    children = centroids.shape[1]
    n = lax.axis_size("dp")
    groups = lax.axis_size("grp")
    chunk = parents // CAP
    per_owner = chunk // 2 // groups
    shape = (4, 8, 2) if n == 64 else (1, n // 2, 2)

    dma = pltpu.SemaphoreType.DMA
    vmem, smem = pltpu.VMEM, pltpu.SMEM
    cells = (CAP, n, children, width)
    ints = (n, 1, LANES)
    bf16, f32, i32 = jnp.bfloat16, jnp.float32, jnp.int32
    by_owner = (CAP, ITERS, groups, per_owner + 1, children, LANES)
    return pl.pallas_call(
        functools.partial(kernel, n, groups, shape),
        out_shape=jax.ShapeDtypeStruct(centroids.shape, bf16),
        in_specs=[pl.BlockSpec(memory_space=pl.ANY)] * 4,
        out_specs=pl.BlockSpec(memory_space=vmem),
        scratch_shapes=[
            vmem((1, parents), i32),
            vmem((1, parents), i32),
            vmem((n, LANES), i32),
            vmem(ints, i32),
            vmem((3 + CAP, 1, parents), i32),
            smem((3 + CAP, 1, parents), i32),
            vmem((1, 1, parents), i32),
            smem((1, 1, parents), i32),
            vmem((parents, block, width), bf16),
            vmem((parents, children, width), bf16),
            vmem(ints, i32),
            smem(ints, i32),
            vmem(cells, bf16),
            vmem(cells, bf16),
            vmem(cells[1:], bf16),
            vmem(cells, bf16),
            vmem((CAP * n, children, width), bf16),
            vmem((2 * chunk, children, width), bf16),
            vmem(by_owner, f32),
            vmem(by_owner, f32),
            vmem((CAP, ITERS, groups, per_owner, children, LANES), bf16),
            vmem((groups, CAP * per_owner, LANES), f32),
            vmem((groups, CAP * per_owner, LANES), f32),
            vmem((CAP * per_owner, LANES), f32),
            dma((6 + shape[1] // 2,)),
            pltpu.SemaphoreType.REGULAR((shape[1] // 2 - 1,)),
            dma, dma((shape[1] // 2,)),
            dma((CAP,)), dma((CAP,)), dma((CAP,)), dma((CAP,)),
            dma, dma,
            dma((CAP, ITERS)), dma((CAP, ITERS)), dma((CAP, ITERS)), dma((CAP, ITERS)),
        ],
        compiler_params=pltpu.CompilerParams(
            collective_id=0, has_side_effects=True, vmem_limit_bytes=28 << 20
        ),
        name="refine",
    )(
        *(
            pltpu.with_memory_space_constraint(value, pltpu.HBM)
            for value in (
                parent_slot.reshape(1, parents),
                lengths.reshape(1, parents),
                embeddings,
                centroids,
            )
        )
    )


def solution(mesh):
    return jax.shard_map(
        on_device,
        mesh=mesh,
        in_specs=(P("dp", None, "grp"), P("dp"), P("dp"), P("dp", None, "grp")),
        out_specs=P("dp", None, "grp"),
        check_vma=False,
    )
```
